32 devices in a mesh: batch: 2 (over x), seq: 4 (over y, core), mp: 4 (over z).
Axes of the slice: x: 2, y: 2, z: 4, core: 2. Of those that a mesh axis runs over, the one named last changes fastest.
Arguments:
- context: bfloat16 [1024, 6144], P(('batch', 'seq'), 'mp'), may hold values from -0.25 to 0.25
- cotangent: bfloat16 [1024, 6144], P(('batch', 'seq'), 'mp'), may hold values from -6 to 6
- out_weight: bfloat16 [6144, 6144], P(None, 'mp'), may hold values from -0.078125 to 0.078125
Outputs:
- grad_weight: float32 [6144, 6144], P(('batch', 'seq'), 'mp')
- grad_context: bfloat16 [1024, 6144], P(('batch', 'seq'), 'mp')
The draws below stay inside these ranges and needn't reach their ends.
All inputs are finite; a program needn't handle non-finite values.
Results may differ from the reference program's by a relative error of at most 0.001.
Values may be sent and summed in bfloat16 or wider, within the bound.
A program may use at most 64 MiB of HBM per device.

```python
import jax
import jax.numpy as jnp
from jax import lax

D = 6144
TOKENS = 1024


def strengthened(values, key, source, target, shards_of, factor):
    def block_of(dim):
        return (jnp.arange(values.shape[dim]) // (values.shape[dim] // shards_of)).reshape((-1,) + (1,) * (values.ndim - 1 - dim))

    near = jax.random.permutation(key, shards_of)[block_of(target)]
    other_side = (block_of(target) + shards_of // 2) % shards_of
    return jnp.where((block_of(source) == near) | (block_of(source) == other_side), factor * values, values)


def block_levels(stream_key, shape, pieces, least, largest):
    def one(dim, parts):
        heights = jax.random.uniform(jax.random.fold_in(jax.random.fold_in(stream_key, 6), dim), (parts,), jnp.float32, least / len(pieces), largest / len(pieces))
        return jnp.repeat(jnp.exp(heights), shape[dim] // parts).reshape((-1,) + (1,) * (len(shape) - dim - 1))

    gain = one(*pieces[0])
    for cut in pieces[1:]:
        gain = gain * one(*cut)
    return gain


def scatter_about(stream_key, dims, scale, limit, split=(), held_as=jnp.bfloat16):
    loudness = block_levels(stream_key, dims, split, -0.22, 0.18) if split else 1.0
    result = jax.random.normal(stream_key, dims, jnp.float32) * scale * loudness
    return jnp.minimum(jnp.maximum(result, -limit), limit).astype(held_as)


def gaussian_with(key, shape, scale, most, pieces, heavy, kind=jnp.bfloat16):
    entries = scale * jax.random.normal(key, shape, jnp.float32)
    if pieces:
        entries = entries * block_levels(key, shape, pieces, -0.22, 0.18)
    return jnp.clip(strengthened(entries, jax.random.fold_in(key, 3), *heavy), -most, most).astype(kind)


def setup_inputs(seed: int = 0) -> dict:
    splits = jax.random.split(jax.random.key(seed), 4)
    return {
        "context": gaussian_with(splits[0], (TOKENS, D), (1 / TOKENS ** 0.5), 0.25, ((0, 8), (1, 4)), (0, 1, 8, 2.0)),
        "cotangent": scatter_about(splits[1], (TOKENS, D), 1.0, 6.0, ((0, 8), (1, 4))),
        "out_weight": scatter_about(splits[2], (D, D), D ** -0.5, 0.078125, ((1, 4),)),
    }


def reference(context, cotangent, out_weight):
    grad_weight = lax.dot_general(context, cotangent, (((0,), (0,)), ((), ())), preferred_element_type=jnp.float32)
    grad_context = lax.dot_general(cotangent, out_weight, (((1,), (1,)), ((), ())), preferred_element_type=jnp.float32)
    return grad_weight, grad_context.astype(jnp.bfloat16)
```

```python
import functools

import jax
import jax.numpy as jnp
from jax import lax
from jax.experimental import pallas as pl
from jax.experimental.pallas import tpu as pltpu
from jax.sharding import PartitionSpec as P

MESH = pl.DeviceIdType.MESH
CHUNKS = 4
SPREAD = 240.0
SMALL = 1.2e-38


def tile_of(width):
    return 256 if width % 256 == 0 else 128


def kernel(
    B, S, M,
    ctx, cot, w, gw, gc,
    zctx, cotall, ctxall, ctxt, part, code, size, rup, sup, rdn, sdn, wbuf,
    wsem, zr, zu, zd, cs, cr, ks, kf, kr, pus, pds, pur, pdr,
):
    G = B * S
    Q = G // M
    T, width = cot.shape
    C = CHUNKS
    rows = T // C
    half = S // 2
    b, s, m = lax.axis_index("batch"), lax.axis_index("seq"), lax.axis_index("mp")
    bs = b * S + s
    parity = lax.rem(s, 2)
    partner = (b, s + 1 - 2 * parity, m)
    partner_bs = b * S + s + 1 - 2 * parity
    above, below = (b, s, m + 1), (b, s, m - 1)
    depth = ctxall.shape[2]
    flat = len(ctx.shape) == 2

    def lines(c):
        return pl.ds(pl.multiple_of(c * rows, rows), rows)

    def piece_of(ref, h, c):
        return ref.at[lines(c), pl.ds(h * depth, depth)] if flat else ref.at[h, lines(c)]

    def part_of(ref, c):
        return ref.at[lines(c), :] if flat else ref.at[:, lines(c), :]

    def plane(index):
        return (index // S, lax.rem(index, S), m)

    def remote(src, dst, send, recv, device):
        return pltpu.make_async_remote_copy(
            src_ref=src, dst_ref=dst, send_sem=send, recv_sem=recv,
            device_id=device, device_id_type=MESH,
        )

    low = 2 * m < M

    def target(position):
        return jnp.where(low, M - 1 - position, position)

    def load(position):
        k = target(position)
        return pltpu.make_async_copy(
            w.at[pl.ds(k * width, width), :], wbuf.at[position % 2], wsem.at[position % 2]
        )

    load(0).start()
    own_cot = pltpu.make_async_copy(cot, cotall.at[bs], kr.at[bs])
    own_cot.start()

    barrier = pltpu.get_barrier_semaphore()
    for d in range(1, G):
        pl.semaphore_signal(
            barrier, inc=1, device_id=plane(lax.rem(bs + d, G)), device_id_type=MESH
        )

    @pl.when(m > 0)
    def _():
        pl.semaphore_signal(barrier, inc=1, device_id=below, device_id_type=MESH)

    @pl.when(m < M - 1)
    def _():
        pl.semaphore_signal(barrier, inc=1, device_id=above, device_id_type=MESH)

    edge = (m == 0) | (m == M - 1)

    @pl.when(edge)
    def _():
        pl.semaphore_wait(barrier, G)

    @pl.when(jnp.logical_not(edge))
    def _():
        pl.semaphore_wait(barrier, G + 1)

    def ctx_up(src, mm, c):
        return remote(part_of(src, c), part_of(zctx.at[mm], c), zu.at[mm, c], zr.at[mm, c], above)

    def ctx_down(src, mm, c):
        return remote(part_of(src, c), part_of(zctx.at[mm], c), zd.at[mm, c], zr.at[mm, c], below)

    def hand_out(src, mm, c):
        for h in range(Q):
            dest = mm * Q + h
            place = ctxall.at[bs, lines(c)]

            @pl.when(dest != bs)
            def _():
                remote(piece_of(src, h, c), place, cs.at[dest, c], cr.at[bs, c], plane(dest)).start()

            @pl.when(dest == bs)
            def _():
                pltpu.make_async_copy(piece_of(src, h, c), place, cr.at[bs, c]).start()

    for c in range(C):
        @pl.when(m < M - 1)
        def _():
            ctx_up(ctx, m, c).start()

        @pl.when(m > 0)
        def _():
            ctx_down(ctx, m, c).start()

    def cot_send(dq):
        q = lax.rem(b * half + s // 2 + dq, B * half)
        dest = (q // half, lax.rem(q, half) * 2 + parity, m)
        return remote(cot, cotall.at[bs], ks.at[dq], kr.at[bs], dest)

    def cot_partner():
        return remote(cot, cotall.at[bs], ks.at[0], kr.at[bs], partner)

    def cot_from(dq):
        q = lax.rem(b * half + s // 2 + dq, B * half)
        return (q // half) * S + lax.rem(q, half) * 2 + parity

    def cot_forward(dq):
        j = cot_from(dq)
        return remote(cotall.at[j], cotall.at[j], kf.at[dq], kr.at[j], partner)

    cot_partner().start()
    for dq in range(1, B * half):
        cot_send(dq).start()
    for c in range(C):
        hand_out(ctx, m, c)

    span = tile_of(width)

    def columns(t):
        return pl.ds(pl.multiple_of(t * span, span), span)

    ups = (above, pus, pur, rup, sup)
    downs = (below, pds, pdr, rdn, sdn)

    def sums(way, k, c):
        device, send, recv, rcode, rsize = way
        return (
            remote(code.at[k, lines(c), :], rcode.at[k, lines(c), :], send.at[k, c, 0], recv.at[k, c, 0], device),
            remote(size.at[k, c], rsize.at[k, c], send.at[k, c, 1], recv.at[k, c, 1], device),
        )

    def send_sum(way, k, c):
        @pl.loop(0, width // span)
        def _(t):
            cols = columns(t)
            value = part[k, lines(c), cols]
            far = jnp.abs(value)
            top = jnp.max(far, axis=0, keepdims=True)
            usable = top > SMALL
            unit = jnp.where(usable, 1.0 / jnp.where(usable, top, 1.0), 0.0)
            coded = jnp.exp2(far * unit * SPREAD - SPREAD / 2)
            code[k, lines(c), cols] = jnp.where(value < 0, -coded, coded).astype(jnp.bfloat16)
            size[k, c, :, cols] = top * (1.0 / SPREAD)

        for copy in sums(way, k, c):
            copy.start()

    def take_sum(way, k, c):
        for copy in sums(way, k, c):
            copy.wait_recv()

        @pl.loop(0, width // span)
        def _(t):
            cols = columns(t)
            coded = way[3][k, lines(c), cols].astype(jnp.float32)
            far = jnp.log2(jnp.abs(coded)) + SPREAD / 2
            part[k, lines(c), cols] += jnp.where(coded < 0, -far, far) * way[4][k, c, :, cols]

    def product(position):
        k = target(position)
        load(position).wait()
        if position + 1 < M:
            load(position + 1).start()

        @pl.loop(0, width // span)
        def _(t):
            cols = columns(t)
            part[k, :, cols] = lax.dot_general(
                cotall[bs], wbuf[position % 2, cols, :],
                (((1,), (1,)), ((), ())), preferred_element_type=jnp.float32,
            )

    own_cot.wait()
    for position in range(M):
        product(position)

    def climb(t, c):
        @pl.when(t < m)
        def _():
            mm = m - 1 - t
            ctx_up(zctx.at[mm], mm, c).wait_recv()

            @pl.when(m < M - 1)
            def _():
                ctx_up(zctx.at[mm], mm, c).start()

            hand_out(zctx.at[mm], mm, c)

        @pl.when(t >= m)
        def _():
            k = M - 1 - t + m

            @pl.when(m > 0)
            def _():
                take_sum(ups, k, c)

            @pl.when(k > m)
            def _():
                send_sum(ups, k, c)

    def descend(t, c):
        left = M - 1 - m

        @pl.when(t < left)
        def _():
            mm = m + 1 + t
            ctx_down(zctx.at[mm], mm, c).wait_recv()

            @pl.when(m > 0)
            def _():
                ctx_down(zctx.at[mm], mm, c).start()

            hand_out(zctx.at[mm], mm, c)

        @pl.when(t >= left)
        def _():
            k = t - left

            @pl.when(m < M - 1)
            def _():
                take_sum(downs, k, c)

            @pl.when(k < m)
            def _():
                send_sum(downs, k, c)

    def steps(first, last):
        @pl.loop(first, last)
        def _(n):
            t, c = n // C, lax.rem(n, C)
            climb(t, c)
            descend(t, c)

    def cot_forwards():
        for dq in range(1, B * half):
            j = cot_from(dq)
            remote(cotall.at[j], cotall.at[j], kf.at[dq], kr.at[j], partner).wait_recv()
            cot_forward(dq).start()

    def cot_arrived():
        remote(cotall.at[partner_bs], cotall.at[partner_bs], ks.at[0], kr.at[partner_bs], partner).wait_recv()
        for dq in range(1, B * half):
            j = cot_from(dq) + 1 - 2 * parity
            remote(cotall.at[j], cotall.at[j], kf.at[dq], kr.at[j], partner).wait_recv()

    gspan = tile_of(width)

    def weight(c):
        piece = pl.ds(c * rows, rows)
        for d in range(1, G):
            j = lax.rem(bs + d, G)
            place = ctxall.at[j, piece]
            remote(place, place, cs.at[j, c], cr.at[j, c], partner).wait_recv()
        place = ctxall.at[bs, piece]
        pltpu.make_async_copy(place, place, cr.at[bs, c]).wait()
        ctxt[...] = ctxall[:, piece, :].reshape(G * rows, depth).T

        @pl.loop(0, width // gspan)
        def _(t):
            cols = pl.ds(pl.multiple_of(t * gspan, gspan), gspan)
            term = jnp.dot(
                ctxt[...], cotall[:, piece, cols].reshape(G * rows, gspan),
                preferred_element_type=jnp.float32,
            )
            if c == 0:
                gw[:, cols] = term
            else:
                gw[:, cols] += term

    end = M * C
    steps(0, end // 2)
    cot_forwards()
    steps(end // 2, end - C + 1)
    cot_arrived()
    weight(0)
    steps(end - C + 1, end - 1)
    weight(1)
    steps(end - 1, end)
    gc[...] = part[m].astype(gc.dtype)
    for c in range(2, C):
        weight(c)

    @pl.loop(0, C)
    def _(c):
        for mm in range(M):
            @pl.when((m < M - 1) & (mm <= m))
            def _():
                ctx_up(ctx, mm, c).wait_send()

            @pl.when((m > 0) & (mm >= m))
            def _():
                ctx_down(ctx, mm, c).wait_send()

            @pl.when(mm > m)
            def _():
                for copy in sums(ups, mm, c):
                    copy.wait_send()

            @pl.when(mm < m)
            def _():
                for copy in sums(downs, mm, c):
                    copy.wait_send()

        for dest in range(G):
            @pl.when(dest != bs)
            def _():
                remote(piece_of(ctx, 0, c), ctxall.at[bs, lines(c)], cs.at[dest, c], cr.at[bs, c], partner).wait_send()

    cot_partner().wait_send()
    for dq in range(1, B * half):
        cot_send(dq).wait_send()
        cot_forward(dq).wait_send()


def shards(context, cotangent, out_weight):
    B, S, M = lax.axis_size("batch"), lax.axis_size("seq"), lax.axis_size("mp")
    G = B * S
    C = CHUNKS
    T, width = cotangent.shape
    Q = G // M
    F = context.shape[1] // Q
    pieces = context
    if F % 128:
        pieces = jnp.stack([context[:, h * F : (h + 1) * F] for h in range(Q)])
    pairs = B * (S // 2)
    dma = pltpu.SemaphoreType.DMA
    vmem = pl.BlockSpec(memory_space=pltpu.VMEM)
    hbm = pl.BlockSpec(memory_space=pltpu.HBM)
    codes = pltpu.VMEM((M, T, width), jnp.bfloat16)
    sizes = pltpu.VMEM((M, C, 1, width), jnp.float32)
    return pl.pallas_call(
        functools.partial(kernel, B, S, M),
        out_shape=(
            jax.ShapeDtypeStruct((F, width), jnp.float32),
            jax.ShapeDtypeStruct((T, context.shape[1]), jnp.bfloat16),
        ),
        in_specs=[hbm, hbm, hbm],
        out_specs=(vmem, vmem),
        scratch_shapes=[
            pltpu.VMEM((M, *pieces.shape), jnp.bfloat16),
            pltpu.VMEM((G, T, width), jnp.bfloat16),
            pltpu.VMEM((G, T, F), jnp.bfloat16),
            pltpu.VMEM((F, G * T // C), jnp.bfloat16),
            pltpu.VMEM((M, T, width), jnp.float32),
            codes, sizes, codes, sizes, codes, sizes,
            pltpu.VMEM((2, width, width), jnp.bfloat16),
            dma((2,)), dma((M, C)), dma((M, C)), dma((M, C)),
            dma((G, C)), dma((G, C)), dma((pairs,)), dma((pairs,)), dma((G,)),
            *[dma((M, C, 2))] * 4,
        ],
        compiler_params=pltpu.CompilerParams(collective_id=0, has_side_effects=True, vmem_limit_bytes=46 * 1024 * 1024),
        name="output_projection_backward",
    )(pieces, cotangent, out_weight)


def solution(mesh):
    return jax.shard_map(
        shards,
        mesh=mesh,
        in_specs=(P(("batch", "seq"), "mp"), P(("batch", "seq"), "mp"), P(None, "mp")),
        out_specs=(P(("batch", "seq"), "mp"), P(("batch", "seq"), "mp")),
        check_vma=False,
    )
```

```python
import functools

import jax
import jax.numpy as jnp
from jax import lax
from jax.experimental import pallas as pl
from jax.experimental.pallas import tpu as pltpu
from jax.sharding import PartitionSpec as P

MESH = pl.DeviceIdType.MESH
CHUNKS = 2
SPREAD = 240.0
SMALL = 1.2e-38


def tile_of(width):
    return 256 if width % 256 == 0 else 128


def kernel(
    B, S, M,
    ctx, cot, w, gw, ctxt, cotall, gc,
    zctx, ctxall, part, code, size, rup, sup, rdn, sdn, wbuf,
    wsem, zr, zu, zd, cs, cr, ks, kf, kr, pus, pds, pur, pdr,
):
    G = B * S
    Q = G // M
    T, width = cot.shape
    C = CHUNKS
    rows = T // C
    half = S // 2
    b, s, m = lax.axis_index("batch"), lax.axis_index("seq"), lax.axis_index("mp")
    bs = b * S + s
    parity = lax.rem(s, 2)
    partner = (b, s + 1 - 2 * parity, m)
    partner_bs = b * S + s + 1 - 2 * parity
    above, below = (b, s, m + 1), (b, s, m - 1)
    depth = ctxall.shape[2]
    flat = len(ctx.shape) == 2

    def lines(c):
        return pl.ds(pl.multiple_of(c * rows, rows), rows)

    def piece_of(ref, h, c):
        return ref.at[lines(c), pl.ds(h * depth, depth)] if flat else ref.at[h, lines(c)]

    def part_of(ref, c):
        return ref.at[lines(c), :] if flat else ref.at[:, lines(c), :]

    def plane(index):
        return (index // S, lax.rem(index, S), m)

    def remote(src, dst, send, recv, device):
        return pltpu.make_async_remote_copy(
            src_ref=src, dst_ref=dst, send_sem=send, recv_sem=recv,
            device_id=device, device_id_type=MESH,
        )

    low = 2 * m < M

    def target(position):
        return jnp.where(low, M - 1 - position, position)

    def load(position):
        k = target(position)
        return pltpu.make_async_copy(
            w.at[pl.ds(k * width, width), :], wbuf.at[position % 2], wsem.at[position % 2]
        )

    load(0).start()
    own_cot = pltpu.make_async_copy(cot, cotall.at[bs], kr.at[bs])
    own_cot.start()

    barrier = pltpu.get_barrier_semaphore()
    for d in range(1, G):
        pl.semaphore_signal(
            barrier, inc=1, device_id=plane(lax.rem(bs + d, G)), device_id_type=MESH
        )

    @pl.when(m > 0)
    def _():
        pl.semaphore_signal(barrier, inc=1, device_id=below, device_id_type=MESH)

    @pl.when(m < M - 1)
    def _():
        pl.semaphore_signal(barrier, inc=1, device_id=above, device_id_type=MESH)

    edge = (m == 0) | (m == M - 1)

    @pl.when(edge)
    def _():
        pl.semaphore_wait(barrier, G)

    @pl.when(jnp.logical_not(edge))
    def _():
        pl.semaphore_wait(barrier, G + 1)

    def ctx_up(src, mm, c):
        return remote(part_of(src, c), part_of(zctx.at[mm], c), zu.at[mm, c], zr.at[mm, c], above)

    def ctx_down(src, mm, c):
        return remote(part_of(src, c), part_of(zctx.at[mm], c), zd.at[mm, c], zr.at[mm, c], below)

    def hand_out(src, mm, c):
        for h in range(Q):
            dest = mm * Q + h
            place = ctxall.at[bs, lines(c)]

            @pl.when(dest != bs)
            def _():
                remote(piece_of(src, h, c), place, cs.at[dest, c], cr.at[bs, c], plane(dest)).start()

            @pl.when(dest == bs)
            def _():
                pltpu.make_async_copy(piece_of(src, h, c), place, cr.at[bs, c]).start()

    for c in range(C):
        @pl.when(m < M - 1)
        def _():
            ctx_up(ctx, m, c).start()

        @pl.when(m > 0)
        def _():
            ctx_down(ctx, m, c).start()

    def cot_send(dq):
        q = lax.rem(b * half + s // 2 + dq, B * half)
        dest = (q // half, lax.rem(q, half) * 2 + parity, m)
        return remote(cot, cotall.at[bs], ks.at[dq], kr.at[bs], dest)

    def cot_partner():
        return remote(cot, cotall.at[bs], ks.at[0], kr.at[bs], partner)

    def cot_from(dq):
        q = lax.rem(b * half + s // 2 + dq, B * half)
        return (q // half) * S + lax.rem(q, half) * 2 + parity

    def cot_forward(dq):
        j = cot_from(dq)
        return remote(cotall.at[j], cotall.at[j], kf.at[dq], kr.at[j], partner)

    cot_partner().start()
    for dq in range(1, B * half):
        cot_send(dq).start()
    for c in range(C):
        hand_out(ctx, m, c)

    span = tile_of(width)
    broad = 512 if width % 512 == 0 else span
    lanes = size.shape[3] * broad // width

    def folded(top):
        parts = [top[:, i : i + lanes] for i in range(0, broad, lanes)]
        return functools.reduce(jnp.maximum, parts)

    def spread(top):
        return jnp.concatenate([top] * (broad // lanes), axis=1)

    def columns(t):
        return pl.ds(pl.multiple_of(t * span, span), span)

    ups = (above, pus, pur, rup, sup)
    downs = (below, pds, pdr, rdn, sdn)

    def sums(way, k, c):
        device, send, recv, rcode, rsize = way
        return (
            remote(code.at[k, lines(c), :], rcode.at[k, lines(c), :], send.at[k, c, 0], recv.at[k, c, 0], device),
            remote(size.at[k, c], rsize.at[k, c], send.at[k, c, 1], recv.at[k, c, 1], device),
        )

    def send_sum(way, k, c):
        @pl.loop(0, width // broad)
        def _(t):
            cols = pl.ds(pl.multiple_of(t * broad, broad), broad)
            value = part[k, lines(c), cols]
            far = jnp.abs(value)
            top = folded(jnp.max(far, axis=0, keepdims=True))
            usable = top > SMALL
            unit = jnp.where(usable, 1.0 / jnp.where(usable, top, 1.0), 0.0)
            coded = jnp.exp2(far * spread(unit) * SPREAD - SPREAD / 2)
            code[k, lines(c), cols] = jnp.where(value < 0, -coded, coded).astype(jnp.bfloat16)
            size[k, c, :, pl.ds(pl.multiple_of(t * lanes, lanes), lanes)] = top * (1.0 / SPREAD)

        for copy in sums(way, k, c):
            copy.start()

    def take_sum(way, k, c):
        for copy in sums(way, k, c):
            copy.wait_recv()

        @pl.loop(0, width // broad)
        def _(t):
            cols = pl.ds(pl.multiple_of(t * broad, broad), broad)
            coded = way[3][k, lines(c), cols].astype(jnp.float32)
            far = jnp.log2(jnp.abs(coded)) + SPREAD / 2
            unit = way[4][k, c, :, pl.ds(pl.multiple_of(t * lanes, lanes), lanes)]
            part[k, lines(c), cols] += jnp.where(coded < 0, -far, far) * spread(unit)

    def product(position):
        k = target(position)
        load(position).wait()
        if position + 1 < M:
            load(position + 1).start()

        @pl.loop(0, width // span)
        def _(t):
            cols = columns(t)
            part[k, :, cols] = lax.dot_general(
                cotall[bs], wbuf[position % 2, cols, :],
                (((1,), (1,)), ((), ())), preferred_element_type=jnp.float32,
            )

    own_cot.wait()
    product(0)

    def climb(t, c):
        @pl.when(t < m)
        def _():
            mm = m - 1 - t
            ctx_up(zctx.at[mm], mm, c).wait_recv()

            @pl.when(m < M - 1)
            def _():
                ctx_up(zctx.at[mm], mm, c).start()

            hand_out(zctx.at[mm], mm, c)

        @pl.when(t >= m)
        def _():
            k = M - 1 - t + m

            @pl.when(m > 0)
            def _():
                take_sum(ups, k, c)

            @pl.when(k > m)
            def _():
                send_sum(ups, k, c)

    def descend(t, c):
        left = M - 1 - m

        @pl.when(t < left)
        def _():
            mm = m + 1 + t
            ctx_down(zctx.at[mm], mm, c).wait_recv()

            @pl.when(m > 0)
            def _():
                ctx_down(zctx.at[mm], mm, c).start()

            hand_out(zctx.at[mm], mm, c)

        @pl.when(t >= left)
        def _():
            k = t - left

            @pl.when(m < M - 1)
            def _():
                take_sum(downs, k, c)

            @pl.when(k < m)
            def _():
                send_sum(downs, k, c)

    def steps(first, last):
        @pl.loop(first, last)
        def _(n):
            t, c = n // C, lax.rem(n, C)
            climb(t, c)
            descend(t, c)

    def cot_forwards():
        for dq in range(1, B * half):
            j = cot_from(dq)
            remote(cotall.at[j], cotall.at[j], kf.at[dq], kr.at[j], partner).wait_recv()
            cot_forward(dq).start()

    def cot_arrived():
        remote(cotall.at[partner_bs], cotall.at[partner_bs], ks.at[0], kr.at[partner_bs], partner).wait_recv()
        for dq in range(1, B * half):
            j = cot_from(dq) + 1 - 2 * parity
            remote(cotall.at[j], cotall.at[j], kf.at[dq], kr.at[j], partner).wait_recv()

    gspan = tile_of(width)

    def weight(c):
        piece = pl.ds(c * rows, rows)
        for d in range(1, G):
            j = lax.rem(bs + d, G)
            place = ctxall.at[j, piece]
            remote(place, place, cs.at[j, c], cr.at[j, c], partner).wait_recv()
        place = ctxall.at[bs, piece]
        pltpu.make_async_copy(place, place, cr.at[bs, c]).wait()
        ctxt[...] = ctxall[:, piece, :].reshape(G * rows, depth).T
        if c == C - 1:
            return

        @pl.loop(0, width // gspan)
        def _(t):
            cols = pl.ds(pl.multiple_of(t * gspan, gspan), gspan)
            term = jnp.dot(
                ctxt[...], cotall[:, piece, cols].reshape(G * rows, gspan),
                preferred_element_type=jnp.float32,
            )
            if c == 0:
                gw[:, cols] = term
            else:
                gw[:, cols] += term

    end = M * C
    for position in range(1, M):
        steps(position - 1, position)
        product(position)
    steps(M - 1, end // 2)
    cot_forwards()
    steps(end // 2, end - 1)
    cot_arrived()
    for c in range(C - 1):
        weight(c)
    steps(end - 1, end)
    gc[...] = part[m].astype(gc.dtype)
    weight(C - 1)

    @pl.loop(0, C)
    def _(c):
        for mm in range(M):
            @pl.when((m < M - 1) & (mm <= m))
            def _():
                ctx_up(ctx, mm, c).wait_send()

            @pl.when((m > 0) & (mm >= m))
            def _():
                ctx_down(ctx, mm, c).wait_send()

            @pl.when(mm > m)
            def _():
                for copy in sums(ups, mm, c):
                    copy.wait_send()

            @pl.when(mm < m)
            def _():
                for copy in sums(downs, mm, c):
                    copy.wait_send()

        for dest in range(G):
            @pl.when(dest != bs)
            def _():
                remote(piece_of(ctx, 0, c), ctxall.at[bs, lines(c)], cs.at[dest, c], cr.at[bs, c], partner).wait_send()

    cot_partner().wait_send()
    for dq in range(1, B * half):
        cot_send(dq).wait_send()
        cot_forward(dq).wait_send()


def finish(rows, total, ctxt, cotall, sums, gw, gc, whole, sent):
    G, T, width = cotall.shape
    span = tile_of(width)
    copies = [pltpu.make_async_copy(sums, gc, sent.at[width // span])]
    copies[0].start()
    for t in range(width // span):
        cols = pl.ds(t * span, span)
        whole[:, cols] = total[:, cols] + jnp.dot(
            ctxt[...], cotall[:, T - rows :, cols].reshape(G * rows, span),
            preferred_element_type=jnp.float32,
        )
        copies.append(pltpu.make_async_copy(whole.at[:, cols], gw.at[:, cols], sent.at[t]))
        copies[-1].start()
    for copy in copies:
        copy.wait()


def shards(context, cotangent, out_weight):
    B, S, M = lax.axis_size("batch"), lax.axis_size("seq"), lax.axis_size("mp")
    G = B * S
    C = CHUNKS
    T, width = cotangent.shape
    Q = G // M
    F = context.shape[1] // Q
    pieces = context
    if F % 128:
        pieces = jnp.stack([context[:, h * F : (h + 1) * F] for h in range(Q)])
    pairs = B * (S // 2)
    dma = pltpu.SemaphoreType.DMA
    vmem = pl.BlockSpec(memory_space=pltpu.VMEM)
    hbm = pl.BlockSpec(memory_space=pltpu.HBM)
    codes = pltpu.VMEM((M, T, width), jnp.bfloat16)
    groups = width // 512 if width % 512 == 0 else width // tile_of(width)
    sizes = pltpu.VMEM((M, C, 1, groups * 128), jnp.float32)
    held = lambda array: pltpu.with_memory_space_constraint(array, pltpu.HBM)
    near = lambda array: pltpu.with_memory_space_constraint(array, pltpu.VMEM)
    sums = pl.pallas_call(
        functools.partial(kernel, B, S, M),
        out_shape=(
            pltpu.VMEM((F, width), jnp.float32),
            pltpu.VMEM((F, G * T // C), jnp.bfloat16),
            pltpu.VMEM((G, T, width), jnp.bfloat16),
            pltpu.VMEM((T, context.shape[1]), jnp.bfloat16),
        ),
        in_specs=[hbm, hbm, hbm],
        out_specs=(vmem,) * 4,
        scratch_shapes=[
            pltpu.VMEM((M, *pieces.shape), jnp.bfloat16),
            pltpu.VMEM((G, T, F), jnp.bfloat16),
            pltpu.VMEM((M, T, width), jnp.float32),
            codes, sizes, codes, sizes, codes, sizes,
            pltpu.VMEM((2, width, width), jnp.bfloat16),
            dma((2,)), dma((M, C)), dma((M, C)), dma((M, C)),
            dma((G, C)), dma((G, C)), dma((pairs,)), dma((pairs,)), dma((G,)),
            *[dma((M, C, 2))] * 4,
        ],
        compiler_params=pltpu.CompilerParams(collective_id=0, has_side_effects=True, vmem_limit_bytes=40 * 1024 * 1024),
        name="output_projection_backward",
    )(held(pieces), held(cotangent), held(out_weight))
    return pl.pallas_call(
        functools.partial(finish, T // C),
        out_shape=(
            jax.ShapeDtypeStruct((F, width), jnp.float32),
            jax.ShapeDtypeStruct((T, context.shape[1]), jnp.bfloat16),
        ),
        in_specs=[vmem] * 4,
        out_specs=(hbm, hbm),
        scratch_shapes=[
            pltpu.VMEM((F, width), jnp.float32),
            dma((width // tile_of(width) + 1,)),
        ],
        compiler_params=pltpu.CompilerParams(vmem_limit_bytes=12 * 1024 * 1024),
        name="last_patches",
    )(*map(near, sums))


def solution(mesh):
    return jax.shard_map(
        shards,
        mesh=mesh,
        in_specs=(P(("batch", "seq"), "mp"), P(("batch", "seq"), "mp"), P(None, "mp")),
        out_specs=(P(("batch", "seq"), "mp"), P(("batch", "seq"), "mp")),
        check_vma=False,
    )
```

```python
import functools

import jax
import jax.numpy as jnp
from jax import lax
from jax.experimental import pallas as pl
from jax.experimental.pallas import tpu as pltpu
from jax.sharding import PartitionSpec as P

MESH = pl.DeviceIdType.MESH
CHUNKS = 2
PIECES = 2
LEAD = 2
SPREAD = 240.0
SMALL = 1.2e-38


def tile_of(width):
    return 256 if width % 256 == 0 else 128


def kernel(
    B, S, M,
    ctx, cot, w, gw, ctxt, cotall, gc,
    zctx, ctxall, part, code, size, rup, sup, rdn, sdn, wbuf,
    wsem, zr, zu, zd, cs, cr, ks, kf, kr, pus, pds, pur, pdr,
):
    G = B * S
    Q = G // M
    T, width = cot.shape
    C = CHUNKS
    rows = T // C
    E = C * PIECES
    some = T // E
    half = S // 2
    b, s, m = lax.axis_index("batch"), lax.axis_index("seq"), lax.axis_index("mp")
    bs = b * S + s
    parity = lax.rem(s, 2)
    partner = (b, s + 1 - 2 * parity, m)
    partner_bs = b * S + s + 1 - 2 * parity
    above, below = (b, s, m + 1), (b, s, m - 1)
    depth = ctxall.shape[2]
    flat = len(ctx.shape) == 2

    def lines(c):
        return pl.ds(pl.multiple_of(c * rows, rows), rows)

    def few(e):
        return pl.ds(pl.multiple_of(e * some, some), some)

    def piece_of(ref, h, e):
        return ref.at[few(e), pl.ds(h * depth, depth)] if flat else ref.at[h, few(e)]

    def part_of(ref, e):
        return ref.at[few(e), :] if flat else ref.at[:, few(e), :]

    def plane(index):
        return (index // S, lax.rem(index, S), m)

    def remote(src, dst, send, recv, device):
        return pltpu.make_async_remote_copy(
            src_ref=src, dst_ref=dst, send_sem=send, recv_sem=recv,
            device_id=device, device_id_type=MESH,
        )

    low = 2 * m < M

    def target(position):
        return jnp.where(low, M - 1 - position, position)

    def load(position):
        k = target(position)
        return pltpu.make_async_copy(
            w.at[pl.ds(k * width, width), :], wbuf.at[position % 2], wsem.at[position % 2]
        )

    load(0).start()
    own_cot = pltpu.make_async_copy(cot, cotall.at[bs], kr.at[bs])
    own_cot.start()

    barrier = pltpu.get_barrier_semaphore()
    for d in range(1, G):
        pl.semaphore_signal(
            barrier, inc=1, device_id=plane(lax.rem(bs + d, G)), device_id_type=MESH
        )

    @pl.when(m > 0)
    def _():
        pl.semaphore_signal(barrier, inc=1, device_id=below, device_id_type=MESH)

    @pl.when(m < M - 1)
    def _():
        pl.semaphore_signal(barrier, inc=1, device_id=above, device_id_type=MESH)

    edge = (m == 0) | (m == M - 1)

    @pl.when(edge)
    def _():
        pl.semaphore_wait(barrier, G)

    @pl.when(jnp.logical_not(edge))
    def _():
        pl.semaphore_wait(barrier, G + 1)

    def ctx_up(src, mm, e):
        return remote(part_of(src, e), part_of(zctx.at[mm], e), zu.at[mm, e], zr.at[mm, e], above)

    def ctx_down(src, mm, e):
        return remote(part_of(src, e), part_of(zctx.at[mm], e), zd.at[mm, e], zr.at[mm, e], below)

    def hand_out(src, mm, e):
        for h in range(Q):
            dest = mm * Q + h
            place = ctxall.at[bs, few(e)]

            @pl.when(dest != bs)
            def _():
                remote(piece_of(src, h, e), place, cs.at[dest, e], cr.at[bs, e], plane(dest)).start()

            @pl.when(dest == bs)
            def _():
                pltpu.make_async_copy(piece_of(src, h, e), place, cr.at[bs, e]).start()

    def located(place, n):
        hops = jnp.int32(0)
        for _ in range(M - 2):
            after = n - LEAD
            mixed = after < 2 * (E - LEAD)
            odd = mixed & (lax.rem(after, 2) == 1)
            mine = (place == 0) | (n < LEAD) | odd
            own = jnp.where((place == 0) | (n < LEAD), n, LEAD + after // 2)
            passed = jnp.where(mixed, after // 2, after - (E - LEAD))
            n = jnp.where(mine, jnp.where(place == 0, n, own), passed)
            hops = jnp.where(mine, hops, hops + 1)
            place = jnp.where(mine, 0, place - 1)
        return hops, n

    for e in range(E):
        @pl.when((m < M - 1) & ((m == 0) | (e < LEAD)))
        def _():
            ctx_up(ctx, m, e).start()

        @pl.when((m > 0) & ((m == M - 1) | (e < LEAD)))
        def _():
            ctx_down(ctx, m, e).start()

    def cot_send(dq):
        q = lax.rem(b * half + s // 2 + dq, B * half)
        dest = (q // half, lax.rem(q, half) * 2 + parity, m)
        return remote(cot, cotall.at[bs], ks.at[dq], kr.at[bs], dest)

    def cot_partner():
        return remote(cot, cotall.at[bs], ks.at[0], kr.at[bs], partner)

    def cot_from(dq):
        q = lax.rem(b * half + s // 2 + dq, B * half)
        return (q // half) * S + lax.rem(q, half) * 2 + parity

    def cot_forward(dq):
        j = cot_from(dq)
        return remote(cotall.at[j], cotall.at[j], kf.at[dq], kr.at[j], partner)

    cot_partner().start()
    for dq in range(1, B * half):
        cot_send(dq).start()
    for e in range(E):
        hand_out(ctx, m, e)

    span = tile_of(width)
    broad = 512 if width % 512 == 0 else span
    lanes = size.shape[3] * broad // width

    def folded(top):
        parts = [top[:, i : i + lanes] for i in range(0, broad, lanes)]
        return functools.reduce(jnp.maximum, parts)

    def spread(top):
        return jnp.concatenate([top] * (broad // lanes), axis=1)

    def columns(t):
        return pl.ds(pl.multiple_of(t * span, span), span)

    ups = (above, pus, pur, rup, sup)
    downs = (below, pds, pdr, rdn, sdn)

    def sums(way, k, c):
        device, send, recv, rcode, rsize = way
        return (
            remote(code.at[k, lines(c), :], rcode.at[k, lines(c), :], send.at[k, c, 0], recv.at[k, c, 0], device),
            remote(size.at[k, c], rsize.at[k, c], send.at[k, c, 1], recv.at[k, c, 1], device),
        )

    def send_sum(way, k, c):
        @pl.loop(0, width // broad)
        def _(t):
            cols = pl.ds(pl.multiple_of(t * broad, broad), broad)
            value = part[k, lines(c), cols]
            far = jnp.abs(value)
            top = folded(jnp.max(far, axis=0, keepdims=True))
            usable = top > SMALL
            unit = jnp.where(usable, 1.0 / jnp.where(usable, top, 1.0), 0.0)
            coded = jnp.exp2(far * spread(unit) * SPREAD - SPREAD / 2)
            code[k, lines(c), cols] = jnp.where(value < 0, -coded, coded).astype(jnp.bfloat16)
            size[k, c, :, pl.ds(pl.multiple_of(t * lanes, lanes), lanes)] = top * (1.0 / SPREAD)

        for copy in sums(way, k, c):
            copy.start()

    def take_sum(way, k, c):
        for copy in sums(way, k, c):
            copy.wait_recv()

        @pl.loop(0, width // broad)
        def _(t):
            cols = pl.ds(pl.multiple_of(t * broad, broad), broad)
            coded = way[3][k, lines(c), cols].astype(jnp.float32)
            far = jnp.log2(jnp.abs(coded)) + SPREAD / 2
            unit = way[4][k, c, :, pl.ds(pl.multiple_of(t * lanes, lanes), lanes)]
            part[k, lines(c), cols] += jnp.where(coded < 0, -far, far) * spread(unit)

    def product(position):
        k = target(position)
        load(position).wait()
        if position + 1 < M:
            load(position + 1).start()

        @pl.loop(0, width // span)
        def _(t):
            cols = columns(t)
            part[k, :, cols] = lax.dot_general(
                cotall[bs], wbuf[position % 2, cols, :],
                (((1,), (1,)), ((), ())), preferred_element_type=jnp.float32,
            )

    own_cot.wait()
    product(0)

    def climb(n):
        q = n - m * E

        @pl.when(q < 0)
        def _():
            hops, e = located(m - 1, n)
            mm = m - 1 - hops
            ctx_up(zctx.at[mm], mm, e).wait_recv()

            @pl.when(m < M - 1)
            def _():
                ctx_up(zctx.at[mm], mm, e).start()

                @pl.when(n + LEAD < E)
                def _():
                    ctx_up(ctx, m, n + LEAD).start()

            hand_out(zctx.at[mm], mm, e)

        @pl.when((q >= 0) & (lax.rem(n, PIECES) == PIECES - 1))
        def _():
            k = M - 1 - q // E
            c = lax.rem(q, E) // PIECES

            @pl.when(m > 0)
            def _():
                take_sum(ups, k, c)

            @pl.when(k > m)
            def _():
                send_sum(ups, k, c)

    def descend(n):
        left = M - 1 - m
        q = n - left * E

        @pl.when(q < 0)
        def _():
            hops, e = located(left - 1, n)
            mm = m + 1 + hops
            ctx_down(zctx.at[mm], mm, e).wait_recv()

            @pl.when(m > 0)
            def _():
                ctx_down(zctx.at[mm], mm, e).start()

                @pl.when(n + LEAD < E)
                def _():
                    ctx_down(ctx, m, n + LEAD).start()

            hand_out(zctx.at[mm], mm, e)

        @pl.when((q >= 0) & (lax.rem(n, PIECES) == PIECES - 1))
        def _():
            k = q // E
            c = lax.rem(q, E) // PIECES

            @pl.when(m < M - 1)
            def _():
                take_sum(downs, k, c)

            @pl.when(k < m)
            def _():
                send_sum(downs, k, c)

    def steps(start, stop):
        @pl.loop(start, stop)
        def _(n):
            climb(n)
            descend(n)

    def cot_forwards():
        for dq in range(1, B * half):
            j = cot_from(dq)
            remote(cotall.at[j], cotall.at[j], kf.at[dq], kr.at[j], partner).wait_recv()
            cot_forward(dq).start()

    def cot_arrived():
        remote(cotall.at[partner_bs], cotall.at[partner_bs], ks.at[0], kr.at[partner_bs], partner).wait_recv()
        for dq in range(1, B * half):
            j = cot_from(dq) + 1 - 2 * parity
            remote(cotall.at[j], cotall.at[j], kf.at[dq], kr.at[j], partner).wait_recv()

    gspan = tile_of(width)

    def weight(c):
        piece = pl.ds(c * rows, rows)
        @pl.loop(c * PIECES, (c + 1) * PIECES)
        def _(e):
            for d in range(1, G):
                j = lax.rem(bs + d, G)
                place = ctxall.at[j, few(e)]
                remote(place, place, cs.at[j, e], cr.at[j, e], partner).wait_recv()
            place = ctxall.at[bs, few(e)]
            pltpu.make_async_copy(place, place, cr.at[bs, e]).wait()

        ctxt[...] = ctxall[:, piece, :].reshape(G * rows, depth).T
        if c == C - 1:
            return

        @pl.loop(0, width // gspan)
        def _(t):
            cols = pl.ds(pl.multiple_of(t * gspan, gspan), gspan)
            term = jnp.dot(
                ctxt[...], cotall[:, piece, cols].reshape(G * rows, gspan),
                preferred_element_type=jnp.float32,
            )
            if c == 0:
                gw[:, cols] = term
            else:
                gw[:, cols] += term

    end = M * E
    at = 0
    for position in range(1, M):
        steps(at, position * E // 2)
        at = position * E // 2
        product(position)
    if at < end // 2:
        steps(at, end // 2)
        at = end // 2
    cot_forwards()
    steps(at, end - 1)
    cot_arrived()
    for c in range(C - 1):
        weight(c)
    steps(end - 1, end)
    gc[...] = part[m].astype(gc.dtype)
    weight(C - 1)

    @pl.loop(0, C)
    def _(c):
        for mm in range(M):
            @pl.when(mm > m)
            def _():
                for copy in sums(ups, mm, c):
                    copy.wait_send()

            @pl.when(mm < m)
            def _():
                for copy in sums(downs, mm, c):
                    copy.wait_send()

    @pl.loop(0, E)
    def _(e):
        for mm in range(M):
            @pl.when((m < M - 1) & (mm <= m))
            def _():
                ctx_up(ctx, mm, e).wait_send()

            @pl.when((m > 0) & (mm >= m))
            def _():
                ctx_down(ctx, mm, e).wait_send()

        for dest in range(G):
            @pl.when(dest != bs)
            def _():
                remote(piece_of(ctx, 0, e), ctxall.at[bs, few(e)], cs.at[dest, e], cr.at[bs, e], partner).wait_send()

    cot_partner().wait_send()
    for dq in range(1, B * half):
        cot_send(dq).wait_send()
        cot_forward(dq).wait_send()


def finish(rows, total, ctxt, cotall, sums, gw, gc, whole, sent):
    G, T, width = cotall.shape
    span = tile_of(width)
    copies = [pltpu.make_async_copy(sums, gc, sent.at[width // span])]
    copies[0].start()
    for t in range(width // span):
        cols = pl.ds(t * span, span)
        whole[:, cols] = total[:, cols] + jnp.dot(
            ctxt[...], cotall[:, T - rows :, cols].reshape(G * rows, span),
            preferred_element_type=jnp.float32,
        )
        copies.append(pltpu.make_async_copy(whole.at[:, cols], gw.at[:, cols], sent.at[t]))
        copies[-1].start()
    for copy in copies:
        copy.wait()


def shards(context, cotangent, out_weight):
    B, S, M = lax.axis_size("batch"), lax.axis_size("seq"), lax.axis_size("mp")
    G = B * S
    C = CHUNKS
    T, width = cotangent.shape
    Q = G // M
    F = context.shape[1] // Q
    pieces = context
    if F % 128:
        pieces = jnp.stack([context[:, h * F : (h + 1) * F] for h in range(Q)])
    E = C * PIECES
    pairs = B * (S // 2)
    dma = pltpu.SemaphoreType.DMA
    vmem = pl.BlockSpec(memory_space=pltpu.VMEM)
    hbm = pl.BlockSpec(memory_space=pltpu.HBM)
    codes = pltpu.VMEM((M, T, width), jnp.bfloat16)
    groups = width // 512 if width % 512 == 0 else width // tile_of(width)
    sizes = pltpu.VMEM((M, C, 1, groups * 128), jnp.float32)
    held = lambda array: pltpu.with_memory_space_constraint(array, pltpu.HBM)
    near = lambda array: pltpu.with_memory_space_constraint(array, pltpu.VMEM)
    sums = pl.pallas_call(
        functools.partial(kernel, B, S, M),
        out_shape=(
            pltpu.VMEM((F, width), jnp.float32),
            pltpu.VMEM((F, G * T // C), jnp.bfloat16),
            pltpu.VMEM((G, T, width), jnp.bfloat16),
            pltpu.VMEM((T, context.shape[1]), jnp.bfloat16),
        ),
        in_specs=[hbm, hbm, hbm],
        out_specs=(vmem,) * 4,
        scratch_shapes=[
            pltpu.VMEM((M, *pieces.shape), jnp.bfloat16),
            pltpu.VMEM((G, T, F), jnp.bfloat16),
            pltpu.VMEM((M, T, width), jnp.float32),
            codes, sizes, codes, sizes, codes, sizes,
            pltpu.VMEM((2, width, width), jnp.bfloat16),
            dma((2,)), dma((M, E)), dma((M, E)), dma((M, E)),
            dma((G, E)), dma((G, E)), dma((pairs,)), dma((pairs,)), dma((G,)),
            *[dma((M, C, 2))] * 4,
        ],
        compiler_params=pltpu.CompilerParams(collective_id=0, has_side_effects=True, vmem_limit_bytes=40 * 1024 * 1024),
        name="output_projection_backward",
    )(held(pieces), held(cotangent), held(out_weight))
    return pl.pallas_call(
        functools.partial(finish, T // C),
        out_shape=(
            jax.ShapeDtypeStruct((F, width), jnp.float32),
            jax.ShapeDtypeStruct((T, context.shape[1]), jnp.bfloat16),
        ),
        in_specs=[vmem] * 4,
        out_specs=(hbm, hbm),
        scratch_shapes=[
            pltpu.VMEM((F, width), jnp.float32),
            dma((width // tile_of(width) + 1,)),
        ],
        compiler_params=pltpu.CompilerParams(vmem_limit_bytes=12 * 1024 * 1024),
        name="last_patches",
    )(*map(near, sums))


def solution(mesh):
    return jax.shard_map(
        shards,
        mesh=mesh,
        in_specs=(P(("batch", "seq"), "mp"), P(("batch", "seq"), "mp"), P(None, "mp")),
        out_specs=(P(("batch", "seq"), "mp"), P(("batch", "seq"), "mp")),
        check_vma=False,
    )
```

```python
import functools

import jax
import jax.numpy as jnp
from jax import lax
from jax.experimental import pallas as pl
from jax.experimental.pallas import tpu as pltpu
from jax.sharding import PartitionSpec as P

MESH = pl.DeviceIdType.MESH
CHUNKS = 2
PIECES = 2
LEAD = 2
SPREAD = 240.0
SMALL = 1.2e-38


def tile_of(width):
    return 256 if width % 256 == 0 else 128


def kernel(
    B, S, M,
    ctx, cot, w, gw, ctxt, cotall, gc,
    zctx, ctxall, part, code, size, rup, sup, rdn, sdn, wbuf,
    ready, wsem, zr, zu, zd, cs, cr, ks, kf, kr, pus, pds, pur, pdr,
):
    G = B * S
    Q = G // M
    T, width = cot.shape
    C = CHUNKS
    rows = T // C
    E = C * PIECES
    some = T // E
    half = S // 2
    b, s, m = lax.axis_index("batch"), lax.axis_index("seq"), lax.axis_index("mp")
    bs = b * S + s
    parity = lax.rem(s, 2)
    partner = (b, s + 1 - 2 * parity, m)
    partner_bs = b * S + s + 1 - 2 * parity
    above, below = (b, s, m + 1), (b, s, m - 1)
    depth = ctxall.shape[2]
    flat = len(ctx.shape) == 2

    def lines(c):
        return pl.ds(pl.multiple_of(c * rows, rows), rows)

    def few(e):
        return pl.ds(pl.multiple_of(e * some, some), some)

    def piece_of(ref, h, e):
        return ref.at[few(e), pl.ds(h * depth, depth)] if flat else ref.at[h, few(e)]

    def part_of(ref, e):
        return ref.at[few(e), :] if flat else ref.at[:, few(e), :]

    def plane(index):
        return (index // S, lax.rem(index, S), m)

    def remote(src, dst, send, recv, device):
        return pltpu.make_async_remote_copy(
            src_ref=src, dst_ref=dst, send_sem=send, recv_sem=recv,
            device_id=device, device_id_type=MESH,
        )

    low = 2 * m < M

    def target(position):
        return jnp.where(low, M - 1 - position, position)

    def load(position):
        k = target(position)
        return pltpu.make_async_copy(
            w.at[pl.ds(k * width, width), :], wbuf.at[position % 2], wsem.at[position % 2]
        )

    load(0).start()
    own_cot = pltpu.make_async_copy(cot, cotall.at[bs], kr.at[bs])
    own_cot.start()

    barrier = pltpu.get_barrier_semaphore()
    for d in range(1, B):
        pl.semaphore_signal(
            barrier, inc=1, device_id=(lax.rem(b + d, B), s, m), device_id_type=MESH
        )
    for d in range(1, S):
        pl.semaphore_signal(
            barrier, inc=1, device_id=(b, lax.rem(s + d, S), m), device_id_type=MESH
        )

    @pl.when(m > 0)
    def _():
        pl.semaphore_signal(barrier, inc=1, device_id=below, device_id_type=MESH)

    @pl.when(m < M - 1)
    def _():
        pl.semaphore_signal(barrier, inc=1, device_id=above, device_id_type=MESH)

    edge = (m == 0) | (m == M - 1)

    @pl.when(edge)
    def _():
        pl.semaphore_wait(barrier, B + S - 1)

    @pl.when(jnp.logical_not(edge))
    def _():
        pl.semaphore_wait(barrier, B + S)

    def ctx_up(src, mm, e):
        return remote(part_of(src, e), part_of(zctx.at[mm], e), zu.at[mm, e], zr.at[mm, e], above)

    def ctx_down(src, mm, e):
        return remote(part_of(src, e), part_of(zctx.at[mm], e), zd.at[mm, e], zr.at[mm, e], below)

    def hand_out(src, mm, e):
        for h in range(Q):
            dest = mm * Q + h
            place = ctxall.at[bs, few(e)]

            @pl.when(dest != bs)
            def _():
                remote(piece_of(src, h, e), place, cs.at[dest, e], cr.at[bs, e], plane(dest)).start()

            @pl.when(dest == bs)
            def _():
                pltpu.make_async_copy(piece_of(src, h, e), place, cr.at[bs, e]).start()

    def located(place, n):
        hops = jnp.int32(0)
        for _ in range(M - 2):
            after = n - LEAD
            mixed = after < 2 * (E - LEAD)
            odd = mixed & (lax.rem(after, 2) == 1)
            mine = (place == 0) | (n < LEAD) | odd
            own = jnp.where((place == 0) | (n < LEAD), n, LEAD + after // 2)
            passed = jnp.where(mixed, after // 2, after - (E - LEAD))
            n = jnp.where(mine, jnp.where(place == 0, n, own), passed)
            hops = jnp.where(mine, hops, hops + 1)
            place = jnp.where(mine, 0, place - 1)
        return hops, n

    for e in range(E):
        @pl.when((m < M - 1) & ((m == 0) | (e < LEAD)))
        def _():
            ctx_up(ctx, m, e).start()

        @pl.when((m > 0) & ((m == M - 1) | (e < LEAD)))
        def _():
            ctx_down(ctx, m, e).start()

    def cot_send(dq):
        q = lax.rem(b * half + s // 2 + dq, B * half)
        dest = (q // half, lax.rem(q, half) * 2 + parity, m)
        return remote(cot, cotall.at[bs], ks.at[dq], kr.at[bs], dest)

    def cot_partner():
        return remote(cot, cotall.at[bs], ks.at[0], kr.at[bs], partner)

    def cot_from(dq):
        q = lax.rem(b * half + s // 2 + dq, B * half)
        return (q // half) * S + lax.rem(q, half) * 2 + parity

    def cot_forward(dq):
        j = cot_from(dq)
        return remote(cotall.at[j], cotall.at[j], kf.at[dq], kr.at[j], partner)

    for d in range(1, B):
        pl.semaphore_signal(
            ready, inc=1, device_id=(lax.rem(b + d, B), s, m), device_id_type=MESH
        )
    cot_partner().start()
    pl.semaphore_wait(ready, B - 1)
    for dq in range(1, B * half):
        cot_send(dq).start()
    for e in range(E):
        hand_out(ctx, m, e)

    span = tile_of(width)
    broad = 512 if width % 512 == 0 else span
    lanes = size.shape[3] * broad // width

    def folded(top):
        parts = [top[:, i : i + lanes] for i in range(0, broad, lanes)]
        return functools.reduce(jnp.maximum, parts)

    def spread(top):
        return jnp.concatenate([top] * (broad // lanes), axis=1)

    def columns(t):
        return pl.ds(pl.multiple_of(t * span, span), span)

    ups = (above, pus, pur, rup, sup)
    downs = (below, pds, pdr, rdn, sdn)

    def sums(way, k, c):
        device, send, recv, rcode, rsize = way
        return (
            remote(code.at[k, lines(c), :], rcode.at[k, lines(c), :], send.at[k, c, 0], recv.at[k, c, 0], device),
            remote(size.at[k, c], rsize.at[k, c], send.at[k, c, 1], recv.at[k, c, 1], device),
        )

    def send_sum(way, k, c):
        @pl.loop(0, width // broad)
        def _(t):
            cols = pl.ds(pl.multiple_of(t * broad, broad), broad)
            value = part[k, lines(c), cols]
            far = jnp.abs(value)
            top = folded(jnp.max(far, axis=0, keepdims=True))
            usable = top > SMALL
            unit = jnp.where(usable, 1.0 / jnp.where(usable, top, 1.0), 0.0)
            coded = jnp.exp2(far * spread(unit) * SPREAD - SPREAD / 2)
            code[k, lines(c), cols] = jnp.where(value < 0, -coded, coded).astype(jnp.bfloat16)
            size[k, c, :, pl.ds(pl.multiple_of(t * lanes, lanes), lanes)] = top * (1.0 / SPREAD)

        for copy in sums(way, k, c):
            copy.start()

    def take_sum(way, k, c):
        for copy in sums(way, k, c):
            copy.wait_recv()

        @pl.loop(0, width // broad)
        def _(t):
            cols = pl.ds(pl.multiple_of(t * broad, broad), broad)
            coded = way[3][k, lines(c), cols].astype(jnp.float32)
            far = jnp.log2(jnp.abs(coded)) + SPREAD / 2
            unit = way[4][k, c, :, pl.ds(pl.multiple_of(t * lanes, lanes), lanes)]
            part[k, lines(c), cols] += jnp.where(coded < 0, -far, far) * spread(unit)

    def product(position):
        k = target(position)
        load(position).wait()
        if position + 1 < M:
            load(position + 1).start()

        @pl.loop(0, width // span)
        def _(t):
            cols = columns(t)
            part[k, :, cols] = lax.dot_general(
                cotall[bs], wbuf[position % 2, cols, :],
                (((1,), (1,)), ((), ())), preferred_element_type=jnp.float32,
            )

    own_cot.wait()
    product(0)

    def climb(n):
        q = n - m * E

        @pl.when(q < 0)
        def _():
            hops, e = located(m - 1, n)
            mm = m - 1 - hops
            ctx_up(zctx.at[mm], mm, e).wait_recv()

            @pl.when(m < M - 1)
            def _():
                ctx_up(zctx.at[mm], mm, e).start()

                @pl.when(n + LEAD < E)
                def _():
                    ctx_up(ctx, m, n + LEAD).start()

            hand_out(zctx.at[mm], mm, e)

        @pl.when((q >= 0) & (lax.rem(n, PIECES) == PIECES - 1))
        def _():
            k = M - 1 - q // E
            c = lax.rem(q, E) // PIECES

            @pl.when(m > 0)
            def _():
                take_sum(ups, k, c)

            @pl.when(k > m)
            def _():
                send_sum(ups, k, c)

    def descend(n):
        left = M - 1 - m
        q = n - left * E

        @pl.when(q < 0)
        def _():
            hops, e = located(left - 1, n)
            mm = m + 1 + hops
            ctx_down(zctx.at[mm], mm, e).wait_recv()

            @pl.when(m > 0)
            def _():
                ctx_down(zctx.at[mm], mm, e).start()

                @pl.when(n + LEAD < E)
                def _():
                    ctx_down(ctx, m, n + LEAD).start()

            hand_out(zctx.at[mm], mm, e)

        @pl.when((q >= 0) & (lax.rem(n, PIECES) == PIECES - 1))
        def _():
            k = q // E
            c = lax.rem(q, E) // PIECES

            @pl.when(m < M - 1)
            def _():
                take_sum(downs, k, c)

            @pl.when(k < m)
            def _():
                send_sum(downs, k, c)

    def steps(start, stop):
        @pl.loop(start, stop)
        def _(n):
            climb(n)
            descend(n)

    def cot_forwards():
        for dq in range(1, B * half):
            j = cot_from(dq)
            remote(cotall.at[j], cotall.at[j], kf.at[dq], kr.at[j], partner).wait_recv()
            cot_forward(dq).start()

    def cot_arrived():
        remote(cotall.at[partner_bs], cotall.at[partner_bs], ks.at[0], kr.at[partner_bs], partner).wait_recv()
        for dq in range(1, B * half):
            j = cot_from(dq) + 1 - 2 * parity
            remote(cotall.at[j], cotall.at[j], kf.at[dq], kr.at[j], partner).wait_recv()

    gspan = tile_of(width)

    def weight(c):
        piece = pl.ds(c * rows, rows)
        @pl.loop(c * PIECES, (c + 1) * PIECES)
        def _(e):
            for d in range(1, G):
                j = lax.rem(bs + d, G)
                place = ctxall.at[j, few(e)]
                remote(place, place, cs.at[j, e], cr.at[j, e], partner).wait_recv()
            place = ctxall.at[bs, few(e)]
            pltpu.make_async_copy(place, place, cr.at[bs, e]).wait()

        ctxt[...] = ctxall[:, piece, :].reshape(G * rows, depth).T
        if c == C - 1:
            return

        @pl.loop(0, width // gspan)
        def _(t):
            cols = pl.ds(pl.multiple_of(t * gspan, gspan), gspan)
            term = jnp.dot(
                ctxt[...], cotall[:, piece, cols].reshape(G * rows, gspan),
                preferred_element_type=jnp.float32,
            )
            if c == 0:
                gw[:, cols] = term
            else:
                gw[:, cols] += term

    end = M * E
    at = 0
    for position in range(1, M):
        steps(at, position * E // 2)
        at = position * E // 2
        product(position)
    if at < end // 2:
        steps(at, end // 2)
        at = end // 2
    cot_forwards()
    steps(at, end - 1)
    cot_arrived()
    for c in range(C - 1):
        weight(c)
    steps(end - 1, end)
    gc[...] = part[m].astype(gc.dtype)
    weight(C - 1)

    @pl.loop(0, C)
    def _(c):
        for mm in range(M):
            @pl.when(mm > m)
            def _():
                for copy in sums(ups, mm, c):
                    copy.wait_send()

            @pl.when(mm < m)
            def _():
                for copy in sums(downs, mm, c):
                    copy.wait_send()

    @pl.loop(0, E)
    def _(e):
        for mm in range(M):
            @pl.when((m < M - 1) & (mm <= m))
            def _():
                ctx_up(ctx, mm, e).wait_send()

            @pl.when((m > 0) & (mm >= m))
            def _():
                ctx_down(ctx, mm, e).wait_send()

        for dest in range(G):
            @pl.when(dest != bs)
            def _():
                remote(piece_of(ctx, 0, e), ctxall.at[bs, few(e)], cs.at[dest, e], cr.at[bs, e], partner).wait_send()

    cot_partner().wait_send()
    for dq in range(1, B * half):
        cot_send(dq).wait_send()
        cot_forward(dq).wait_send()


def finish(rows, total, ctxt, cotall, sums, gw, gc, whole, sent):
    G, T, width = cotall.shape
    span = tile_of(width)
    copies = [pltpu.make_async_copy(sums, gc, sent.at[width // span])]
    copies[0].start()
    for t in range(width // span):
        cols = pl.ds(t * span, span)
        whole[:, cols] = total[:, cols] + jnp.dot(
            ctxt[...], cotall[:, T - rows :, cols].reshape(G * rows, span),
            preferred_element_type=jnp.float32,
        )
        copies.append(pltpu.make_async_copy(whole.at[:, cols], gw.at[:, cols], sent.at[t]))
        copies[-1].start()
    for copy in copies:
        copy.wait()


def shards(context, cotangent, out_weight):
    B, S, M = lax.axis_size("batch"), lax.axis_size("seq"), lax.axis_size("mp")
    G = B * S
    C = CHUNKS
    T, width = cotangent.shape
    Q = G // M
    F = context.shape[1] // Q
    pieces = context
    if F % 128:
        pieces = jnp.stack([context[:, h * F : (h + 1) * F] for h in range(Q)])
    E = C * PIECES
    pairs = B * (S // 2)
    dma = pltpu.SemaphoreType.DMA
    vmem = pl.BlockSpec(memory_space=pltpu.VMEM)
    hbm = pl.BlockSpec(memory_space=pltpu.HBM)
    codes = pltpu.VMEM((M, T, width), jnp.bfloat16)
    groups = width // 512 if width % 512 == 0 else width // tile_of(width)
    sizes = pltpu.VMEM((M, C, 1, groups * 128), jnp.float32)
    held = lambda array: pltpu.with_memory_space_constraint(array, pltpu.HBM)
    near = lambda array: pltpu.with_memory_space_constraint(array, pltpu.VMEM)
    sums = pl.pallas_call(
        functools.partial(kernel, B, S, M),
        out_shape=(
            pltpu.VMEM((F, width), jnp.float32),
            pltpu.VMEM((F, G * T // C), jnp.bfloat16),
            pltpu.VMEM((G, T, width), jnp.bfloat16),
            pltpu.VMEM((T, context.shape[1]), jnp.bfloat16),
        ),
        in_specs=[hbm, hbm, hbm],
        out_specs=(vmem,) * 4,
        scratch_shapes=[
            pltpu.VMEM((M, *pieces.shape), jnp.bfloat16),
            pltpu.VMEM((G, T, F), jnp.bfloat16),
            pltpu.VMEM((M, T, width), jnp.float32),
            codes, sizes, codes, sizes, codes, sizes,
            pltpu.VMEM((2, width, width), jnp.bfloat16),
            pltpu.SemaphoreType.REGULAR, dma((2,)), dma((M, E)), dma((M, E)), dma((M, E)),
            dma((G, E)), dma((G, E)), dma((pairs,)), dma((pairs,)), dma((G,)),
            *[dma((M, C, 2))] * 4,
        ],
        compiler_params=pltpu.CompilerParams(collective_id=0, has_side_effects=True, vmem_limit_bytes=40 * 1024 * 1024),
        name="output_projection_backward",
    )(held(pieces), held(cotangent), held(out_weight))
    return pl.pallas_call(
        functools.partial(finish, T // C),
        out_shape=(
            jax.ShapeDtypeStruct((F, width), jnp.float32),
            jax.ShapeDtypeStruct((T, context.shape[1]), jnp.bfloat16),
        ),
        in_specs=[vmem] * 4,
        out_specs=(hbm, hbm),
        scratch_shapes=[
            pltpu.VMEM((F, width), jnp.float32),
            dma((width // tile_of(width) + 1,)),
        ],
        compiler_params=pltpu.CompilerParams(vmem_limit_bytes=12 * 1024 * 1024),
        name="last_patches",
    )(*map(near, sums))


def solution(mesh):
    return jax.shard_map(
        shards,
        mesh=mesh,
        in_specs=(P(("batch", "seq"), "mp"), P(("batch", "seq"), "mp"), P(None, "mp")),
        out_specs=(P(("batch", "seq"), "mp"), P(("batch", "seq"), "mp")),
        check_vma=False,
    )
```

```python
import functools

import jax
import jax.numpy as jnp
from jax import lax
from jax.experimental import pallas as pl
from jax.experimental.pallas import tpu as pltpu
from jax.sharding import PartitionSpec as P

MESH = pl.DeviceIdType.MESH
CHUNKS = 2
PIECES = 2
LEAD = 2
SPREAD = 240.0
SMALL = 1.2e-38


def tile_of(width):
    return 256 if width % 256 == 0 else 128


def kernel(
    B, S, M,
    ctx, cot, w, gw, ctxt, cotall, gc,
    zctx, ctxall, part, code, size, rup, sup, rdn, sdn, wbuf,
    ready, wsem, zr, zu, zd, cs, cr, ks, kf, kr, pus, pds, pur, pdr,
):
    G = B * S
    Q = G // M
    T, width = cot.shape
    C = CHUNKS
    rows = T // C
    E = C * PIECES
    some = T // E
    half = S // 2
    b, s, m = lax.axis_index("batch"), lax.axis_index("seq"), lax.axis_index("mp")
    bs = b * S + s
    parity = lax.rem(s, 2)
    partner = (b, s + 1 - 2 * parity, m)
    partner_bs = b * S + s + 1 - 2 * parity
    above, below = (b, s, m + 1), (b, s, m - 1)
    depth = ctxall.shape[2]
    flat = len(ctx.shape) == 2

    def lines(c):
        return pl.ds(pl.multiple_of(c * rows, rows), rows)

    def few(e):
        return pl.ds(pl.multiple_of(e * some, some), some)

    def piece_of(ref, h, e):
        return ref.at[few(e), pl.ds(h * depth, depth)] if flat else ref.at[h, few(e)]

    def part_of(ref, e):
        return ref.at[few(e), :] if flat else ref.at[:, few(e), :]

    def plane(index):
        return (index // S, lax.rem(index, S), m)

    def remote(src, dst, send, recv, device):
        return pltpu.make_async_remote_copy(
            src_ref=src, dst_ref=dst, send_sem=send, recv_sem=recv,
            device_id=device, device_id_type=MESH,
        )

    low = 2 * m < M

    def target(position):
        return jnp.where(low, M - 1 - position, position)

    def load(position):
        k = target(position)
        return pltpu.make_async_copy(
            w.at[pl.ds(k * width, width), :], wbuf.at[position % 2], wsem.at[position % 2]
        )

    load(0).start()
    own_cot = pltpu.make_async_copy(cot, cotall.at[bs], kr.at[bs])
    own_cot.start()

    barrier = pltpu.get_barrier_semaphore()
    for d in range(1, B):
        pl.semaphore_signal(
            barrier, inc=1, device_id=(lax.rem(b + d, B), s, m), device_id_type=MESH
        )
    for d in range(1, S):
        pl.semaphore_signal(
            barrier, inc=1, device_id=(b, lax.rem(s + d, S), m), device_id_type=MESH
        )

    @pl.when(m > 0)
    def _():
        pl.semaphore_signal(barrier, inc=1, device_id=below, device_id_type=MESH)

    @pl.when(m < M - 1)
    def _():
        pl.semaphore_signal(barrier, inc=1, device_id=above, device_id_type=MESH)

    edge = (m == 0) | (m == M - 1)

    @pl.when(edge)
    def _():
        pl.semaphore_wait(barrier, B + S - 1)

    @pl.when(jnp.logical_not(edge))
    def _():
        pl.semaphore_wait(barrier, B + S)

    def ctx_up(src, mm, e):
        return remote(part_of(src, e), part_of(zctx.at[mm], e), zu.at[mm, e], zr.at[mm, e], above)

    def ctx_down(src, mm, e):
        return remote(part_of(src, e), part_of(zctx.at[mm], e), zd.at[mm, e], zr.at[mm, e], below)

    def hand_out(src, mm, e):
        for h in range(Q):
            dest = mm * Q + h
            place = ctxall.at[bs, few(e)]

            @pl.when(dest != bs)
            def _():
                remote(piece_of(src, h, e), place, cs.at[dest, e], cr.at[bs, e], plane(dest)).start()

            @pl.when(dest == bs)
            def _():
                pltpu.make_async_copy(piece_of(src, h, e), place, cr.at[bs, e]).start()

    def located(place, n):
        hops = jnp.int32(0)
        for _ in range(M - 2):
            after = n - LEAD
            mixed = after < 2 * (E - LEAD)
            odd = mixed & (lax.rem(after, 2) == 1)
            mine = (place == 0) | (n < LEAD) | odd
            own = jnp.where((place == 0) | (n < LEAD), n, LEAD + after // 2)
            passed = jnp.where(mixed, after // 2, after - (E - LEAD))
            n = jnp.where(mine, jnp.where(place == 0, n, own), passed)
            hops = jnp.where(mine, hops, hops + 1)
            place = jnp.where(mine, 0, place - 1)
        return hops, n

    for e in range(E):
        @pl.when((m < M - 1) & ((m == 0) | (e < LEAD)))
        def _():
            ctx_up(ctx, m, e).start()

        @pl.when((m > 0) & ((m == M - 1) | (e < LEAD)))
        def _():
            ctx_down(ctx, m, e).start()

    def cot_send(dq):
        q = lax.rem(b * half + s // 2 + dq, B * half)
        dest = (q // half, lax.rem(q, half) * 2 + parity, m)
        return remote(cot, cotall.at[bs], ks.at[dq], kr.at[bs], dest)

    def cot_partner():
        return remote(cot, cotall.at[bs], ks.at[0], kr.at[bs], partner)

    def cot_from(dq):
        q = lax.rem(b * half + s // 2 + dq, B * half)
        return (q // half) * S + lax.rem(q, half) * 2 + parity

    def cot_forward(dq):
        j = cot_from(dq)
        return remote(cotall.at[j], cotall.at[j], kf.at[dq], kr.at[j], partner)

    for d in range(1, B):
        pl.semaphore_signal(
            ready, inc=1, device_id=(lax.rem(b + d, B), s, m), device_id_type=MESH
        )
    cot_partner().start()
    pl.semaphore_wait(ready, B - 1)
    for dq in range(1, B * half):
        cot_send(dq).start()

    span = tile_of(width)
    broad = 512 if width % 512 == 0 else span
    lanes = size.shape[3] * broad // width

    def folded(top):
        parts = [top[:, i : i + lanes] for i in range(0, broad, lanes)]
        return functools.reduce(jnp.maximum, parts)

    def spread(top):
        return jnp.concatenate([top] * (broad // lanes), axis=1)

    def columns(t):
        return pl.ds(pl.multiple_of(t * span, span), span)

    ups = (above, pus, pur, rup, sup)
    downs = (below, pds, pdr, rdn, sdn)

    def sums(way, k, c):
        device, send, recv, rcode, rsize = way
        return (
            remote(code.at[k, lines(c), :], rcode.at[k, lines(c), :], send.at[k, c, 0], recv.at[k, c, 0], device),
            remote(size.at[k, c], rsize.at[k, c], send.at[k, c, 1], recv.at[k, c, 1], device),
        )

    def send_sum(way, k, c):
        @pl.loop(0, width // broad)
        def _(t):
            cols = pl.ds(pl.multiple_of(t * broad, broad), broad)
            value = part[k, lines(c), cols]
            far = jnp.abs(value)
            top = folded(jnp.max(far, axis=0, keepdims=True))
            usable = top > SMALL
            unit = jnp.where(usable, 1.0 / jnp.where(usable, top, 1.0), 0.0)
            coded = jnp.exp2(far * spread(unit) * SPREAD - SPREAD / 2)
            code[k, lines(c), cols] = jnp.where(value < 0, -coded, coded).astype(jnp.bfloat16)
            size[k, c, :, pl.ds(pl.multiple_of(t * lanes, lanes), lanes)] = top * (1.0 / SPREAD)

        for copy in sums(way, k, c):
            copy.start()

    def take_sum(way, k, c):
        for copy in sums(way, k, c):
            copy.wait_recv()

        @pl.loop(0, width // broad)
        def _(t):
            cols = pl.ds(pl.multiple_of(t * broad, broad), broad)
            coded = way[3][k, lines(c), cols].astype(jnp.float32)
            far = jnp.log2(jnp.abs(coded)) + SPREAD / 2
            unit = way[4][k, c, :, pl.ds(pl.multiple_of(t * lanes, lanes), lanes)]
            part[k, lines(c), cols] += jnp.where(coded < 0, -far, far) * spread(unit)

    def product(position):
        k = target(position)
        load(position).wait()
        if position + 1 < M:
            load(position + 1).start()

        @pl.loop(0, width // span)
        def _(t):
            cols = columns(t)
            part[k, :, cols] = lax.dot_general(
                cotall[bs], wbuf[position % 2, cols, :],
                (((1,), (1,)), ((), ())), preferred_element_type=jnp.float32,
            )

    own_cot.wait()
    product(0)

    def climb(n):
        q = n - m * E

        @pl.when(q < 0)
        def _():
            hops, e = located(m - 1, n)
            mm = m - 1 - hops
            ctx_up(zctx.at[mm], mm, e).wait_recv()

            @pl.when(m < M - 1)
            def _():
                ctx_up(zctx.at[mm], mm, e).start()

                @pl.when(n + LEAD < E)
                def _():
                    ctx_up(ctx, m, n + LEAD).start()

            hand_out(zctx.at[mm], mm, e)

        @pl.when((q >= 0) & (lax.rem(n, PIECES) == PIECES - 1))
        def _():
            k = M - 1 - q // E
            c = lax.rem(q, E) // PIECES

            @pl.when(m > 0)
            def _():
                take_sum(ups, k, c)

            @pl.when(k > m)
            def _():
                send_sum(ups, k, c)

    def descend(n):
        left = M - 1 - m
        q = n - left * E

        @pl.when(q < 0)
        def _():
            hops, e = located(left - 1, n)
            mm = m + 1 + hops
            ctx_down(zctx.at[mm], mm, e).wait_recv()

            @pl.when(m > 0)
            def _():
                ctx_down(zctx.at[mm], mm, e).start()

                @pl.when(n + LEAD < E)
                def _():
                    ctx_down(ctx, m, n + LEAD).start()

            hand_out(zctx.at[mm], mm, e)

        @pl.when((q >= 0) & (lax.rem(n, PIECES) == PIECES - 1))
        def _():
            k = q // E
            c = lax.rem(q, E) // PIECES

            @pl.when(m < M - 1)
            def _():
                take_sum(downs, k, c)

            @pl.when(k < m)
            def _():
                send_sum(downs, k, c)

    def steps(start, stop):
        @pl.loop(start, stop)
        def _(n):
            climb(n)
            descend(n)

    def cot_forwards():
        for dq in range(1, B * half):
            j = cot_from(dq)
            remote(cotall.at[j], cotall.at[j], kf.at[dq], kr.at[j], partner).wait_recv()
            cot_forward(dq).start()

    def cot_arrived():
        remote(cotall.at[partner_bs], cotall.at[partner_bs], ks.at[0], kr.at[partner_bs], partner).wait_recv()
        for dq in range(1, B * half):
            j = cot_from(dq) + 1 - 2 * parity
            remote(cotall.at[j], cotall.at[j], kf.at[dq], kr.at[j], partner).wait_recv()

    gspan = tile_of(width)

    def weight(c):
        piece = pl.ds(c * rows, rows)
        @pl.loop(c * PIECES, (c + 1) * PIECES)
        def _(e):
            for d in range(1, G):
                j = lax.rem(bs + d, G)
                place = ctxall.at[j, few(e)]
                remote(place, place, cs.at[j, e], cr.at[j, e], partner).wait_recv()
            place = ctxall.at[bs, few(e)]
            pltpu.make_async_copy(place, place, cr.at[bs, e]).wait()

        ctxt[...] = ctxall[:, piece, :].reshape(G * rows, depth).T

        @pl.loop(0, width // gspan if c < C - 1 else 1)
        def _(t):
            cols = pl.ds(pl.multiple_of(t * gspan, gspan), gspan)
            term = jnp.dot(
                ctxt[...], cotall[:, piece, cols].reshape(G * rows, gspan),
                preferred_element_type=jnp.float32,
            )
            if c == 0:
                gw[:, cols] = term
            else:
                gw[:, cols] += term

    end = M * E
    at = 0
    for position in range(1, M):
        steps(at, position * E // 2)
        at = position * E // 2
        product(position)
        if position == 1:
            for e in range(E):
                hand_out(ctx, m, e)
    if at < end // 2:
        steps(at, end // 2)
        at = end // 2
    cot_forwards()
    steps(at, end - PIECES - 1)
    cot_arrived()
    for c in range(C - 1):
        weight(c)
    steps(end - PIECES - 1, end - 1)
    weight(C - 1)
    steps(end - 1, end)
    gc[...] = part[m].astype(gc.dtype)

    @pl.loop(0, C)
    def _(c):
        for mm in range(M):
            @pl.when(mm > m)
            def _():
                for copy in sums(ups, mm, c):
                    copy.wait_send()

            @pl.when(mm < m)
            def _():
                for copy in sums(downs, mm, c):
                    copy.wait_send()

    @pl.loop(0, E)
    def _(e):
        for mm in range(M):
            @pl.when((m < M - 1) & (mm <= m))
            def _():
                ctx_up(ctx, mm, e).wait_send()

            @pl.when((m > 0) & (mm >= m))
            def _():
                ctx_down(ctx, mm, e).wait_send()

        for dest in range(G):
            @pl.when(dest != bs)
            def _():
                remote(piece_of(ctx, 0, e), ctxall.at[bs, few(e)], cs.at[dest, e], cr.at[bs, e], partner).wait_send()

    cot_partner().wait_send()
    for dq in range(1, B * half):
        cot_send(dq).wait_send()
        cot_forward(dq).wait_send()


def finish(rows, total, ctxt, cotall, sums, gw, gc, whole, sent):
    G, T, width = cotall.shape
    span = tile_of(width)
    copies = [pltpu.make_async_copy(sums, gc, sent.at[width // span])]
    copies[0].start()
    copies.append(pltpu.make_async_copy(total.at[:, :span], gw.at[:, :span], sent.at[0]))
    copies[-1].start()
    for t in range(1, width // span):
        cols = pl.ds(t * span, span)
        whole[:, cols] = total[:, cols] + jnp.dot(
            ctxt[...], cotall[:, T - rows :, cols].reshape(G * rows, span),
            preferred_element_type=jnp.float32,
        )
        copies.append(pltpu.make_async_copy(whole.at[:, cols], gw.at[:, cols], sent.at[t]))
        copies[-1].start()
    for copy in copies:
        copy.wait()


def shards(context, cotangent, out_weight):
    B, S, M = lax.axis_size("batch"), lax.axis_size("seq"), lax.axis_size("mp")
    G = B * S
    C = CHUNKS
    T, width = cotangent.shape
    Q = G // M
    F = context.shape[1] // Q
    pieces = context
    if F % 128:
        pieces = jnp.stack([context[:, h * F : (h + 1) * F] for h in range(Q)])
    E = C * PIECES
    pairs = B * (S // 2)
    dma = pltpu.SemaphoreType.DMA
    vmem = pl.BlockSpec(memory_space=pltpu.VMEM)
    hbm = pl.BlockSpec(memory_space=pltpu.HBM)
    codes = pltpu.VMEM((M, T, width), jnp.bfloat16)
    groups = width // 512 if width % 512 == 0 else width // tile_of(width)
    sizes = pltpu.VMEM((M, C, 1, groups * 128), jnp.float32)
    held = lambda array: pltpu.with_memory_space_constraint(array, pltpu.HBM)
    near = lambda array: pltpu.with_memory_space_constraint(array, pltpu.VMEM)
    sums = pl.pallas_call(
        functools.partial(kernel, B, S, M),
        out_shape=(
            pltpu.VMEM((F, width), jnp.float32),
            pltpu.VMEM((F, G * T // C), jnp.bfloat16),
            pltpu.VMEM((G, T, width), jnp.bfloat16),
            pltpu.VMEM((T, context.shape[1]), jnp.bfloat16),
        ),
        in_specs=[hbm, hbm, hbm],
        out_specs=(vmem,) * 4,
        scratch_shapes=[
            pltpu.VMEM((M, *pieces.shape), jnp.bfloat16),
            pltpu.VMEM((G, T, F), jnp.bfloat16),
            pltpu.VMEM((M, T, width), jnp.float32),
            codes, sizes, codes, sizes, codes, sizes,
            pltpu.VMEM((2, width, width), jnp.bfloat16),
            pltpu.SemaphoreType.REGULAR, dma((2,)), dma((M, E)), dma((M, E)), dma((M, E)),
            dma((G, E)), dma((G, E)), dma((pairs,)), dma((pairs,)), dma((G,)),
            *[dma((M, C, 2))] * 4,
        ],
        compiler_params=pltpu.CompilerParams(collective_id=0, has_side_effects=True, vmem_limit_bytes=40 * 1024 * 1024),
        name="output_projection_backward",
    )(held(pieces), held(cotangent), held(out_weight))
    return pl.pallas_call(
        functools.partial(finish, T // C),
        out_shape=(
            jax.ShapeDtypeStruct((F, width), jnp.float32),
            jax.ShapeDtypeStruct((T, context.shape[1]), jnp.bfloat16),
        ),
        in_specs=[vmem] * 4,
        out_specs=(hbm, hbm),
        scratch_shapes=[
            pltpu.VMEM((F, width), jnp.float32),
            dma((width // tile_of(width) + 1,)),
        ],
        compiler_params=pltpu.CompilerParams(vmem_limit_bytes=12 * 1024 * 1024),
        name="last_patches",
    )(*map(near, sums))


def solution(mesh):
    return jax.shard_map(
        shards,
        mesh=mesh,
        in_specs=(P(("batch", "seq"), "mp"), P(("batch", "seq"), "mp"), P(None, "mp")),
        out_specs=(P(("batch", "seq"), "mp"), P(("batch", "seq"), "mp")),
        check_vma=False,
    )
```
